1024 devices in a mesh: section: 2 (over core), ctx: 32 (over y, x), tp: 16 (over z).
Axes of the slice: x: 4, y: 8, z: 16, core: 2. Of those that a mesh axis runs over, the one named last changes fastest.
Arguments:
- activations: bfloat16 [2, 4096, 4096], P(None, 'ctx', 'tp'), may hold values from -6 to 6
- norm_gain: float32 [2, 4096], P('section'), may hold values from 0.1 to 1.9
- value_projection: bfloat16 [2, 4096, 4096], P('section', None, 'tp'), may hold values from -0.09375 to 0.09375
- short_taps: float32 [2, 3, 3, 4096], P('section', None, None, 'tp'), may hold values from -3 to 3
- long_taps: bfloat16 [2, 256, 128], P('section', 'tp'), may hold values from -0.5 to 0.5
- skip_gain: float32 [2, 4096], P('section', 'tp'), may hold values from -4 to 4
- out_projection: bfloat16 [2, 4096, 4096], P('section', 'tp'), may hold values from -0.09375 to 0.09375
Outputs:
- layer_out: bfloat16 [2, 4096, 4096], P('section', 'ctx', 'tp')
The draws below stay inside these ranges and needn't reach their ends.
All inputs are finite; a program needn't handle non-finite values.
Results may differ from the reference program's by a relative error of at most 0.012.
The reference program's roundings to bfloat16 on the way (of `normed`, `product` and `gated`) count: a program that leaves them out, or rounds other values in their place, can miss the bound.
Values may be sent and summed in bfloat16 or wider, within the bound.
A program may use at most 32 MiB of HBM per device.

```python
import jax
import jax.numpy as jnp
from jax import lax

D = 4096
GROUP_WIDTH = 16
FILT = 128
SHORT = 3
GROUPS = 256
MB = 2
LAYERS = 2
TOKENS = 4096


def level_of(key, shape, cuts, smallest, high):
    loudness = 1.0
    for axis_at, shards_of in cuts:
        draws = jax.random.uniform(jax.random.fold_in(jax.random.fold_in(key, 6), axis_at), (shards_of,), jnp.float32, smallest / len(cuts), high / len(cuts))
        loudness = loudness * jnp.repeat(jnp.exp(draws), shape[axis_at] // shards_of).reshape((-1,) + (1,) * (len(shape) - 1 - axis_at))
    return loudness


def noise(key, shape, spread, most, split=(), held_as=jnp.bfloat16):
    drawn = spread * jax.random.normal(key, shape, jnp.float32)
    if split:
        drawn = drawn * level_of(key, shape, split, -0.22, 0.18)
    return jnp.clip(drawn, -most, most).astype(held_as)


def setup_inputs(seed: int = 0) -> dict:
    keys = jax.random.split(jax.random.key(seed), 8)
    return {
        "activations": noise(keys[0], (MB, TOKENS, D), 1.0, 6.0, ((1, 32), (2, 16))),
        "norm_gain": jnp.clip(1.0 + 0.18 * jax.random.normal(keys[1], (LAYERS, D), jnp.float32), 0.1, 1.9),
        "value_projection": noise(keys[2], (LAYERS, D, D), D ** -0.5, 0.09375, ((0, 2), (2, 16))),
        "short_taps": noise(keys[3], (LAYERS, SHORT, 3, D), 0.6, 3.0, ((0, 2), (3, 16)), jnp.float32),
        "long_taps": noise(keys[4], (LAYERS, GROUPS, FILT), 0.09, 0.5, ((0, 2), (1, 16))),
        "skip_gain": noise(keys[5], (LAYERS, D), 1.0, 4.0, ((0, 2), (1, 16)), jnp.float32),
        "out_projection": noise(keys[6], (LAYERS, D, D), D ** -0.5, 0.09375, ((0, 2), (1, 16))),
    }


EPS = 1e-06

def causal_filter(signal, taps):
    kernel = jnp.repeat(taps.astype(signal.dtype), GROUP_WIDTH, axis=0).T
    padded = jnp.pad(signal, ((FILT - 1, 0), (0, 0)))
    rows = signal.shape[0]

    def add_tap(index, total):
        where = jnp.asarray(index).astype(jnp.int32)
        start = (FILT - 1 - where).astype(jnp.int32)
        piece = lax.dynamic_slice_in_dim(padded, start, rows, 0)
        tap = lax.dynamic_slice_in_dim(kernel, where, 1, 0)
        return total + tap * piece
    return lax.fori_loop(0, FILT, add_tap, jnp.zeros_like(signal))

def one_layer(hidden, gain, weight, short, taps, skip, out_weight):
    hid = hidden.astype(jnp.float32)
    scale = lax.rsqrt(lax.optimization_barrier(jnp.mean(hid * hid, axis=1, keepdims=True)) + EPS)
    normed = lax.optimization_barrier((hid * gain).astype(jnp.bfloat16))
    normed_f = normed.astype(jnp.float32)
    projected = jnp.dot(normed_f, weight.astype(jnp.float32), precision=lax.Precision.HIGHEST) * scale
    values = projected.astype(jnp.bfloat16)
    query = (normed_f * scale).astype(jnp.bfloat16)
    stacked = jnp.stack([query, query, values], axis=1).astype(jnp.float32)
    padded = jnp.pad(stacked, ((2, 0), (0, 0), (0, 0)))
    featured = short[0] * padded[2:] + short[1] * padded[1:-1] + short[2] * padded[:-2]
    product = (featured[:, 1] * featured[:, 2]).astype(jnp.bfloat16)
    product_f = product.astype(jnp.float32)
    mixed = causal_filter(product_f, taps) + skip * product_f
    gated = (featured[:, 0] * mixed).astype(jnp.bfloat16)
    summed = jnp.dot(gated, out_weight, preferred_element_type=jnp.float32)
    return (hid + summed).astype(jnp.bfloat16)

def reference(activations, norm_gain, value_projection, short_taps, long_taps, skip_gain, out_projection):
    results = []
    for micro in range(MB):
        hidden = activations[micro]
        for layer in range(LAYERS):
            hidden = one_layer(hidden, norm_gain[layer], value_projection[layer], short_taps[layer], long_taps[layer], skip_gain[layer], out_projection[layer])
        results.append(hidden)
    return jnp.stack(results)
```

```python
import jax
import jax.numpy as jnp
from jax import lax
from jax.sharding import PartitionSpec as P

EPS = 1e-06


def from_behind(shard, axis, by):
    count = lax.axis_size(axis)
    pairs = [(i, i + by) for i in range(count) if 0 <= i + by < count]
    return lax.ppermute(shard, axis, pairs)


def swapped(array):
    return lax.ppermute(array, "section", [(0, 1), (1, 0)])


def toeplitz(taps, rows):
    groups, filt = taps.shape
    period = 2 * filt
    v = jnp.concatenate([jnp.flip(taps, axis=1), jnp.zeros_like(taps)], axis=1)
    tiled = jnp.tile(v, (1, rows))[:, : rows * (period - 1)]
    return tiled.reshape(groups * rows, period - 1)


def layer(current, gain, flat, short, taps, skip, out_weight):
    rows, local = current.shape
    width = flat.shape[0]
    group_count, filt = taps.shape
    group_width = local // group_count
    column = lax.axis_index("tp") * local
    local_gain = lax.dynamic_slice_in_dim(gain, column, local)
    matrix = toeplitz(taps, rows)
    whole = lax.all_gather(current, "tp", axis=1, tiled=True)
    whole_f = whole.astype(jnp.float32)
    squares = jnp.sum(whole_f * whole_f, axis=1, keepdims=True)
    normed = (whole_f * gain).astype(jnp.bfloat16)
    raw_proj = jnp.dot(normed, flat, preferred_element_type=jnp.float32)
    scale = lax.rsqrt(squares / width + EPS)
    values = (raw_proj * scale).astype(jnp.bfloat16)
    own = current.astype(jnp.float32)
    own_normed = lax.optimization_barrier((own * local_gain).astype(jnp.bfloat16))
    query = (own_normed.astype(jnp.float32) * scale).astype(jnp.bfloat16)
    both = jnp.stack([query, values], axis=0)
    rim = from_behind(both[:, rows - 2 :], "ctx", 1)
    padded = jnp.concatenate([rim, both], axis=1).astype(jnp.float32)

    def featured(index, source):
        p = padded[source]
        return short[0, index] * p[2:] + short[1, index] * p[1:-1] + short[2, index] * p[:-2]

    product = (featured(1, 0) * featured(2, 1)).astype(jnp.bfloat16)
    before = from_behind(product[rows - (filt - 1) :], "ctx", 1)
    extended = jnp.concatenate([before, product], axis=0)
    all_groups = jnp.dot(matrix, extended, preferred_element_type=jnp.float32)
    all_groups = all_groups.reshape(group_count, rows, local)
    group_of = lax.broadcasted_iota(jnp.int32, all_groups.shape, 2) // group_width
    mine = lax.broadcasted_iota(jnp.int32, all_groups.shape, 0) == group_of
    filtered = jnp.sum(jnp.where(mine, all_groups, 0.0), axis=0)
    mixed = filtered + skip * product.astype(jnp.float32)
    gated = (featured(0, 0) * mixed).astype(jnp.bfloat16)
    terms = jnp.dot(gated, out_weight, preferred_element_type=jnp.float32).astype(jnp.bfloat16)
    summed = lax.psum_scatter(terms, "tp", scatter_dimension=1, tiled=True)
    return (own + summed.astype(jnp.float32)).astype(jnp.bfloat16)


def body(
    activations, norm_gain, value_projection, short_taps, long_taps, skip_gain, out_projection
):
    section = lax.axis_index("section")
    first = section == 0
    own = (
        norm_gain[0],
        value_projection[0],
        short_taps[0],
        long_taps[0],
        skip_gain[0],
        out_projection[0],
    )
    other = [swapped(a) for a in own]
    current = lax.dynamic_index_in_dim(activations, section, 0, keepdims=False)
    current = layer(current, *[jnp.where(first, a, b) for a, b in zip(own, other)])
    current = layer(current, *[jnp.where(first, b, a) for a, b in zip(own, other)])
    return current[None]


def solution(mesh):
    in_specs = (
        P(None, "ctx", "tp"),
        P("section", None),
        P("section", None, "tp"),
        P("section", None, None, "tp"),
        P("section", "tp", None),
        P("section", "tp"),
        P("section", "tp", None),
    )
    out_specs = P("section", "ctx", "tp")
    return jax.shard_map(body, mesh=mesh, in_specs=in_specs, out_specs=out_specs, check_vma=False)
```

```python
import jax
import jax.numpy as jnp
from jax import lax
from jax.experimental import pallas as pl
from jax.experimental.pallas import tpu as pltpu
from jax.sharding import PartitionSpec as P

EPS = 1e-06
CHUNKS = 2
TAIL = 16
MESH = pl.DeviceIdType.MESH
F32 = jnp.float32
BF16 = jnp.bfloat16


def kernel(
    ring, chain, rows, local, groups, lag,
    act, par_in, wv_in, wo_in, out,
    whole, par, wv, wo, matrix, conv, acc, ssq, qx, vx, qv, halo, tail, term, sent, got,
    act_sem, par_sem, wv_sem, wo_sem, swap_sem,
    ag_s, ag_r, halo_s, halo_r, rs_s, rs_r,
):
    s = lax.axis_index("section")
    c = lax.axis_index("ctx")
    z = lax.axis_index("tp")
    half = ring // 2
    width = ring * local
    group_width = local // groups
    part = rows // CHUNKS
    on_z = (lax.rem(z + 1, ring), lax.rem(z + ring - 1, ring))
    ahead = lax.rem(c + 1, chain)
    ahead2 = lax.rem(c + 2, chain)
    behind = lax.rem(c + chain - 1, chain)
    behind2 = lax.rem(c + chain - 2, chain)
    taps_at = TAIL
    gain_at = TAIL + groups

    barrier = pltpu.get_barrier_semaphore()
    for there in (
        {"section": 1 - s}, {"tp": on_z[0]}, {"tp": on_z[1]},
        {"ctx": ahead}, {"ctx": ahead2}, {"ctx": behind}, {"ctx": behind2},
    ):
        pl.semaphore_signal(barrier, inc=1, device_id=there, device_id_type=MESH)

    own = pltpu.make_async_copy(act.at[s], whole.at[0, z], act_sem)
    own.start()
    weights = ((wv_in, wv, wv_sem), (par_in, par, par_sem), (wo_in, wo, wo_sem))
    for source, held, sem in weights:
        pltpu.make_async_copy(source, held.at[s], sem.at[s]).start()
    pl.semaphore_wait(barrier, 7)

    def swap(index):
        source, held, sem = weights[index]
        return pltpu.make_async_remote_copy(
            source, held.at[s], swap_sem.at[index], sem.at[s],
            device_id={"section": 1 - s}, device_id_type=MESH,
        )

    def ready(layer, index):
        source, held, sem = weights[index]
        pltpu.make_async_copy(source, held.at[layer], sem.at[layer]).wait()

    def piece(q):
        return pl.ds(q * part, part)

    def origin(d, k):
        return lax.rem(z + ring - k, ring) if d == 0 else lax.rem(z + k, ring)

    def gather(layer, d, k, q, received=False):
        block = whole.at[layer, origin(d, k + 1 if received else k), piece(q)]
        return pltpu.make_async_remote_copy(
            block, block, ag_s.at[layer, d, k, q], ag_r.at[layer, d, k, q],
            device_id={"tp": on_z[d]}, device_id_type=MESH,
        )

    def scatter(layer, d, k, q):
        return pltpu.make_async_remote_copy(
            sent.at[layer, d, k, piece(q)], got.at[layer, d, k, piece(q)],
            rs_s.at[layer, d, k, q], rs_r.at[layer, d, k, q],
            device_id={"tp": on_z[d]}, device_id_type=MESH,
        )

    def halo_copy(layer):
        return pltpu.make_async_remote_copy(
            qv.at[layer], halo.at[layer], halo_s.at[layer, 0], halo_r.at[layer, 0],
            device_id={"ctx": ahead}, device_id_type=MESH,
        )

    def tail_copy(layer):
        return pltpu.make_async_remote_copy(
            qv.at[layer, :, pl.ds(rows - TAIL, TAIL)], tail.at[layer],
            halo_s.at[layer, 1], halo_r.at[layer, 1],
            device_id={"ctx": ahead2}, device_id_type=MESH,
        )

    gathers = (half, half - 1)
    scatters = (half - 1, half)

    own.wait()
    for layer in range(2):
        for q in range(CHUNKS):
            for d in range(2):
                gather(layer, d, 0, q).start()
        if layer == 0:
            for index in range(3):
                swap(index).start()
        acc[...] = jnp.zeros_like(acc)
        ssq[...] = jnp.zeros_like(ssq)

        def project(o, layer=layer):
            x = whole[layer, o].astype(F32)
            squared = x * x
            lanes = squared[:, :128]
            for at in range(128, local, 128):
                lanes = lanes + squared[:, at : at + 128]
            ssq[...] += lanes
            normed = (x * par[layer, pl.ds(gain_at + o, 1), :]).astype(BF16)
            acc[...] += jnp.dot(normed, wv[layer, o], preferred_element_type=F32)

        def build(g, layer=layer):
            row = par[layer, pl.ds(taps_at + g, 1), :]
            base = jnp.broadcast_to(row, (rows, 2 * rows))
            turned = pltpu.roll(base, 0, 1, stride=1, stride_axis=0)
            matrix[g * rows : (g + 1) * rows, :] = turned.astype(BF16)

        pending = [z]
        built = 0
        waited = False
        for k in range(half):
            for q in range(CHUNKS):
                for d in range(2):
                    if k < gathers[d]:
                        gather(layer, d, k, q, received=True).wait_recv()
                        if k + 1 < gathers[d]:
                            gather(layer, d, k + 1, q).start()
            for d in range(2):
                if k < gathers[d]:
                    pending.append(origin(d, k + 1))
            if layer == 0 and k < lag:
                continue
            if not waited:
                ready(layer, 0)
                ready(layer, 1)
                waited = True
            count = 4 if k + 1 < half else len(pending)
            for o in pending[:count]:
                project(o)
            pending = pending[count:]
            goal = groups * (k + 1) // half
            for g in range(built, goal):
                build(g)
            built = goal

        def short(i, which, layer=layer):
            return par[layer, i * 3 + which : i * 3 + which + 1, :]

        def featured(which, x, start, count):
            return (
                short(0, which) * x[start : start + count, :]
                + short(1, which) * x[start - 1 : start - 1 + count, :]
                + short(2, which) * x[start - 2 : start - 2 + count, :]
            )

        scale = lax.rsqrt(jnp.sum(ssq[...], axis=1, keepdims=True) / width + EPS)
        values = (acc[...] * scale).astype(BF16)
        normed = (whole[layer, z].astype(F32) * par[layer, pl.ds(gain_at + z, 1), :]).astype(BF16)
        query = (normed.astype(F32) * scale).astype(BF16)
        qv[layer, 1] = values
        qv[layer, 0] = query
        halo_copy(layer).start()
        tail_copy(layer).start()
        qx[TAIL + rows :, :] = query.astype(F32)
        vx[TAIL + rows :, :] = values.astype(F32)
        halo_copy(layer).wait_recv()
        tail_copy(layer).wait_recv()
        for index, x in ((0, qx), (1, vx)):
            x[TAIL : TAIL + rows, :] = jnp.where(c > 0, halo[layer, index].astype(F32), 0.0)
            x[:TAIL, :] = jnp.where(c > 1, tail[layer, index].astype(F32), 0.0)
        product = (
            featured(1, qx, TAIL, 2 * rows) * featured(2, vx, TAIL, 2 * rows)
        ).astype(BF16)
        conv[...] = jnp.dot(matrix[...], product, preferred_element_type=F32)
        group_of = lax.broadcasted_iota(jnp.int32, (rows, local), 1) // group_width
        filtered = conv[:rows, :]
        for g in range(1, groups):
            filtered = jnp.where(group_of == g, conv[g * rows : (g + 1) * rows, :], filtered)
        skip = par[layer, 9:10, :]
        mixed = filtered + skip * product[rows:, :].astype(F32)
        gated = (featured(0, qx, TAIL + rows, rows) * mixed).astype(BF16)

        if layer == 0:
            ready(0, 2)
        else:
            ready(1, 2)

        def terms(dest, layer=layer, gated=gated):
            columns = pl.ds(pl.multiple_of(dest * local, local), local)
            return jnp.dot(gated, wo[layer, :, columns], preferred_element_type=F32)

        def dest(d, k):
            if d == 0:
                return lax.rem(z + half - 1 - k, ring)
            return lax.rem(z + ring - half + k, ring)

        for d in range(2):
            sent[layer, d, 0] = terms(dest(d, 0)).astype(BF16)
            for q in range(CHUNKS):
                scatter(layer, d, 0, q).start()
        for k in range(1, half):
            for d in range(2):
                if k < scatters[d]:
                    term[d] = terms(dest(d, k))
            for q in range(CHUNKS):
                for d in range(2):
                    if k < scatters[d]:
                        scatter(layer, d, k - 1, q).wait_recv()
                        sent[layer, d, k, piece(q)] = (
                            term[d, piece(q)] + got[layer, d, k - 1, piece(q)].astype(F32)
                        ).astype(BF16)
                        scatter(layer, d, k, q).start()
        term[0] = whole[layer, z].astype(F32)
        term[1] = terms(z)
        for q in range(CHUNKS):
            for d in range(2):
                scatter(layer, d, scatters[d] - 1, q).wait_recv()
            summed = (
                term[1, piece(q)]
                + got[layer, 0, scatters[0] - 1, piece(q)].astype(F32)
                + got[layer, 1, scatters[1] - 1, piece(q)].astype(F32)
            )
            result = (term[0, piece(q)] + summed).astype(BF16)
            if layer == 0:
                whole[1, z, piece(q)] = result
            else:
                out[piece(q), :] = result

    for index in range(3):
        swap(index).wait_send()
    for layer in range(2):
        halo_copy(layer).wait_send()
        tail_copy(layer).wait_send()
        for d in range(2):
            for q in range(CHUNKS):
                for k in range(gathers[d]):
                    gather(layer, d, k, q).wait_send()
                for k in range(scatters[d]):
                    scatter(layer, d, k, q).wait_send()


def body(
    activations, norm_gain, value_projection, short_taps, long_taps, skip_gain, out_projection
):
    ring = lax.axis_size("tp")
    chain = lax.axis_size("ctx")
    rows, local = activations.shape[1:]
    width = value_projection.shape[1]
    groups, filt = long_taps.shape[1:]
    half = ring // 2
    taps = jnp.flip(long_taps[0].astype(F32), axis=1)
    par = jnp.concatenate(
        [
            short_taps[0].reshape(9, local),
            skip_gain,
            jnp.zeros((TAIL - 10, local), F32),
            jnp.pad(taps, ((0, 0), (1, local - 1 - filt))),
            norm_gain.reshape(ring, local),
        ],
        axis=0,
    )
    wv = value_projection.reshape(ring, local, local)
    wo = out_projection.reshape(local, width)
    anywhere = pl.BlockSpec(memory_space=pl.ANY)
    vmem = pltpu.VMEM
    dma = pltpu.SemaphoreType.DMA
    result = pl.pallas_call(
        lambda *refs: kernel(ring, chain, rows, local, groups, min(3, half - 1), *refs),
        name="two_layers",
        out_shape=jax.ShapeDtypeStruct((rows, local), BF16),
        in_specs=[anywhere] * 4,
        out_specs=pl.BlockSpec(memory_space=pltpu.VMEM),
        scratch_shapes=[
            vmem((2, ring, rows, local), BF16),
            vmem((2, *par.shape), F32),
            vmem((2, ring, local, local), BF16),
            vmem((2, local, width), BF16),
            vmem((groups * rows, 2 * rows), BF16),
            vmem((groups * rows, local), F32),
            vmem((rows, local), F32),
            vmem((rows, 128), F32),
            vmem((2 * rows + TAIL, local), F32),
            vmem((2 * rows + TAIL, local), F32),
            vmem((2, 2, rows, local), BF16),
            vmem((2, 2, rows, local), BF16),
            vmem((2, 2, TAIL, local), BF16),
            vmem((2, rows, local), F32),
            vmem((2, 2, half, rows, local), BF16),
            vmem((2, 2, half, rows, local), BF16),
            dma,
            dma((2,)),
            dma((2,)),
            dma((2,)),
            dma((3,)),
            dma((2, 2, half, CHUNKS)),
            dma((2, 2, half, CHUNKS)),
            dma((2, 2)),
            dma((2, 2)),
            dma((2, 2, half, CHUNKS)),
            dma((2, 2, half, CHUNKS)),
        ],
        compiler_params=pltpu.CompilerParams(
            collective_id=0, has_side_effects=True, vmem_limit_bytes=60 * 1024 * 1024
        ),
    )(activations, par, wv, wo)
    return result[None]


def solution(mesh):
    in_specs = (
        P(None, "ctx", "tp"),
        P("section", None),
        P("section", None, "tp"),
        P("section", None, None, "tp"),
        P("section", "tp", None),
        P("section", "tp"),
        P("section", "tp", None),
    )
    out_specs = P("section", "ctx", "tp")
    return jax.shard_map(body, mesh=mesh, in_specs=in_specs, out_specs=out_specs, check_vma=False)
```

```python
import jax
import jax.numpy as jnp
from jax import lax
from jax.experimental import pallas as pl
from jax.experimental.pallas import tpu as pltpu
from jax.sharding import PartitionSpec as P

EPS = 1e-06
CHUNKS = 2
TAIL = 16
MESH = pl.DeviceIdType.MESH
F32 = jnp.float32
BF16 = jnp.bfloat16


def kernel(
    ring, chain, rows, local, groups, lag,
    act, wv_in, gain_in, taps_in, short_in, skip_in, wo_in, out,
    whole, wv, gain, taps, shorts, skips, wo,
    matrix, conv, acc, ssq, qx, vx, qv, halo, tail, term,
    far_out, far_got, near_out, near_got,
    act_sem, hold_sem, swap_sem,
    agf_s, agf_r, agn_s, agn_r, halo_s, halo_r, rsf_s, rsf_r, rsn_s, rsn_r,
):
    s = lax.axis_index("section")
    c = lax.axis_index("ctx")
    z = lax.axis_index("tp")
    half = ring // 2
    stages = half // 2
    width = ring * local
    group_width = local // groups
    part = rows // CHUNKS
    sign = (1, -1)

    def at_z(d, hops):
        return lax.rem(z + ring + sign[d] * hops, ring)

    ahead = lax.rem(c + 1, chain)
    ahead2 = lax.rem(c + 2, chain)
    behind = lax.rem(c + chain - 1, chain)
    behind2 = lax.rem(c + chain - 2, chain)

    barrier = pltpu.get_barrier_semaphore()
    for there in (
        {"section": 1 - s}, {"tp": at_z(0, 1)}, {"tp": at_z(1, 1)}, {"tp": at_z(0, 2)}, {"tp": at_z(1, 2)},
        {"ctx": ahead}, {"ctx": ahead2}, {"ctx": behind}, {"ctx": behind2},
    ):
        pl.semaphore_signal(barrier, inc=1, device_id=there, device_id_type=MESH)

    own = pltpu.make_async_copy(act.at[s], whole.at[0, z], act_sem)
    own.start()
    weights = (
        (wv_in, wv), (gain_in, gain), (taps_in, taps), (short_in, shorts), (skip_in, skips), (wo_in, wo),
    )
    for index, (source, held) in enumerate(weights):
        pltpu.make_async_copy(source, held.at[s], hold_sem.at[index, s]).start()
    pl.semaphore_wait(barrier, 9)

    def swap(index):
        source, held = weights[index]
        return pltpu.make_async_remote_copy(
            source, held.at[s], swap_sem.at[index], hold_sem.at[index, s],
            device_id={"section": 1 - s}, device_id_type=MESH,
        )

    def ready(layer, *indices):
        for index in indices:
            source, held = weights[index]
            pltpu.make_async_copy(source, held.at[layer], hold_sem.at[index, layer]).wait()

    def piece(q):
        return pl.ds(q * part, part)

    def far_in_gather(d, j):
        return 0 <= j < (stages if d == 0 else stages - 1)

    def far_in_scatter(d, i):
        return (0 if d == 0 else 1) <= i < stages

    def gather_far(layer, d, j, q, received=False):
        block = whole.at[layer, at_z(d, -2 * j - (2 if received else 0)), piece(q)]
        return pltpu.make_async_remote_copy(
            block, block, agf_s.at[layer, d, j, q], agf_r.at[layer, d, j, q],
            device_id={"tp": at_z(d, 2)}, device_id_type=MESH,
        )

    def gather_near(layer, d, j, received=False):
        block = whole.at[layer, at_z(d, -2 * j - (1 if received else 0))]
        return pltpu.make_async_remote_copy(
            block, block, agn_s.at[layer, d, j], agn_r.at[layer, d, j],
            device_id={"tp": at_z(d, 1)}, device_id_type=MESH,
        )

    def scatter_far(layer, d, i, q):
        return pltpu.make_async_remote_copy(
            far_out.at[layer, d, i, piece(q)], far_got.at[layer, d, i, piece(q)],
            rsf_s.at[layer, d, i, q], rsf_r.at[layer, d, i, q],
            device_id={"tp": at_z(d, 2)}, device_id_type=MESH,
        )

    def scatter_near(layer, d, i):
        return pltpu.make_async_remote_copy(
            near_out.at[layer, d, i], near_got.at[layer, d, i],
            rsn_s.at[layer, d, i], rsn_r.at[layer, d, i],
            device_id={"tp": at_z(d, 1)}, device_id_type=MESH,
        )

    def halo_copy(layer):
        return pltpu.make_async_remote_copy(
            qv.at[layer], halo.at[layer], halo_s.at[layer, 0], halo_r.at[layer, 0],
            device_id={"ctx": ahead}, device_id_type=MESH,
        )

    def tail_copy(layer):
        return pltpu.make_async_remote_copy(
            qv.at[layer, :, pl.ds(rows - TAIL, TAIL)], tail.at[layer],
            halo_s.at[layer, 1], halo_r.at[layer, 1],
            device_id={"ctx": ahead2}, device_id_type=MESH,
        )

    own.wait()
    for layer in range(2):
        for q in range(CHUNKS):
            for d in range(2):
                if far_in_gather(d, 0):
                    gather_far(layer, d, 0, q).start()
        for d in range(2):
            gather_near(layer, d, 0).start()
        if layer == 0:
            for index in range(6):
                swap(index).start()
        acc[...] = jnp.zeros_like(acc)
        ssq[...] = jnp.zeros_like(ssq)

        def gain_of(o, layer=layer):
            return gain[layer, :, pl.ds(pl.multiple_of(o * local, local), local)]

        def project(o, layer=layer):
            x = whole[layer, o].astype(F32)
            squared = x * x
            lanes = squared[:, :128]
            for at in range(128, local, 128):
                lanes = lanes + squared[:, at : at + 128]
            ssq[...] += lanes
            normed = (x * gain_of(o)).astype(BF16)
            acc[...] += jnp.dot(normed, wv[layer, o], preferred_element_type=F32)

        def build(g, layer=layer):
            base = jnp.broadcast_to(taps[layer, g : g + 1, :], (rows, 2 * rows))
            turned = pltpu.roll(base, 0, 1, stride=1, stride_axis=0)
            matrix[g * rows : (g + 1) * rows, :] = turned.astype(BF16)

        pending = [(z, None)]
        built = 0
        waited = False
        for j in range(stages):
            for q in range(CHUNKS):
                for d in range(2):
                    if far_in_gather(d, j):
                        gather_far(layer, d, j, q, received=True).wait_recv()
                        if far_in_gather(d, j + 1):
                            gather_far(layer, d, j + 1, q).start()
            for d in range(2):
                if far_in_gather(d, j):
                    if j + 1 < stages:
                        gather_near(layer, d, j + 1).start()
                    pending.append((at_z(d, -2 * j - 2), None))
                pending.append((at_z(d, -2 * j - 1), gather_near(layer, d, j, received=True)))
            if layer == 0 and j < lag:
                continue
            if not waited:
                ready(layer, 0, 1, 2)
                waited = True
            count = 8 if j + 1 < stages else len(pending)
            for o, copy in pending[:count]:
                if copy is not None:
                    copy.wait_recv()
                project(o)
            pending = pending[count:]
            goal = groups * (j + 1) // stages
            for g in range(built, goal):
                build(g)
            built = goal

        def short(i, which, layer=layer):
            return shorts[layer, i, which : which + 1, :]

        def featured(which, x, start, count):
            return (
                short(0, which) * x[start : start + count, :]
                + short(1, which) * x[start - 1 : start - 1 + count, :]
                + short(2, which) * x[start - 2 : start - 2 + count, :]
            )

        scale = lax.rsqrt(jnp.sum(ssq[...], axis=1, keepdims=True) / width + EPS)
        values = (acc[...] * scale).astype(BF16)
        normed = (whole[layer, z].astype(F32) * gain_of(z)).astype(BF16)
        query = (normed.astype(F32) * scale).astype(BF16)
        qv[layer, 1] = values
        qv[layer, 0] = query
        halo_copy(layer).start()
        tail_copy(layer).start()
        qx[TAIL + rows :, :] = query.astype(F32)
        vx[TAIL + rows :, :] = values.astype(F32)
        ready(layer, 3, 4)
        halo_copy(layer).wait_recv()
        tail_copy(layer).wait_recv()
        for index, x in ((0, qx), (1, vx)):
            x[TAIL : TAIL + rows, :] = jnp.where(c > 0, halo[layer, index].astype(F32), 0.0)
            x[:TAIL, :] = jnp.where(c > 1, tail[layer, index].astype(F32), 0.0)
        product = (
            featured(1, qx, TAIL, 2 * rows) * featured(2, vx, TAIL, 2 * rows)
        ).astype(BF16)
        conv[...] = jnp.dot(matrix[...], product, preferred_element_type=F32)
        group_of = lax.broadcasted_iota(jnp.int32, (rows, local), 1) // group_width
        filtered = conv[:rows, :]
        for g in range(1, groups):
            filtered = jnp.where(group_of == g, conv[g * rows : (g + 1) * rows, :], filtered)
        mixed = filtered + skips[layer] * product[rows:, :].astype(F32)
        gated = (featured(0, qx, TAIL + rows, rows) * mixed).astype(BF16)
        ready(layer, 5)

        def terms(dest, layer=layer, gated=gated):
            columns = pl.ds(pl.multiple_of(dest * local, local), local)
            return jnp.dot(gated, wo[layer, :, columns], preferred_element_type=F32)

        def send_near(i, layer=layer):
            for d in range(2):
                near_out[layer, d, i] = terms(at_z(d, half - 2 * i - 1)).astype(BF16)
                scatter_near(layer, d, i).start()

        far_out[layer, 0, 0] = terms(at_z(0, half)).astype(BF16)
        for q in range(CHUNKS):
            scatter_far(layer, 0, 0, q).start()
        send_near(0)
        for i in range(1, stages):
            for d in range(2):
                term[d] = terms(at_z(d, half - 2 * i))
            send_near(i)
            for d in (1, 0):
                scatter_near(layer, d, i - 1).wait_recv()
            for q in range(CHUNKS):
                for d in (1, 0):
                    total = term[d, piece(q)] + near_got[layer, d, i - 1, piece(q)].astype(F32)
                    if far_in_scatter(d, i - 1):
                        scatter_far(layer, d, i - 1, q).wait_recv()
                        total = total + far_got[layer, d, i - 1, piece(q)].astype(F32)
                    far_out[layer, d, i, piece(q)] = total.astype(BF16)
                    scatter_far(layer, d, i, q).start()
        term[0] = whole[layer, z].astype(F32)
        term[1] = terms(z)
        for d in range(2):
            scatter_near(layer, d, stages - 1).wait_recv()
        for q in range(CHUNKS):
            summed = term[1, piece(q)]
            for d in range(2):
                summed = summed + near_got[layer, d, stages - 1, piece(q)].astype(F32)
                if far_in_scatter(d, stages - 1):
                    scatter_far(layer, d, stages - 1, q).wait_recv()
                    summed = summed + far_got[layer, d, stages - 1, piece(q)].astype(F32)
            result = (term[0, piece(q)] + summed).astype(BF16)
            if layer == 0:
                whole[1, z, piece(q)] = result
            else:
                out[piece(q), :] = result

    for index in range(6):
        swap(index).wait_send()
    for layer in range(2):
        halo_copy(layer).wait_send()
        tail_copy(layer).wait_send()
        for d in range(2):
            for j in range(stages):
                gather_near(layer, d, j).wait_send()
                scatter_near(layer, d, j).wait_send()
                for q in range(CHUNKS):
                    if far_in_gather(d, j):
                        gather_far(layer, d, j, q).wait_send()
                    if far_in_scatter(d, j):
                        scatter_far(layer, d, j, q).wait_send()


def body(
    activations, norm_gain, value_projection, short_taps, long_taps, skip_gain, out_projection
):
    ring = lax.axis_size("tp")
    chain = lax.axis_size("ctx")
    rows, local = activations.shape[1:]
    width = value_projection.shape[1]
    groups, filt = long_taps.shape[1:]
    stages = ring // 4
    turned = jnp.flip(long_taps[0].astype(F32), axis=1)
    taps = jnp.pad(turned, ((0, 0), (1, local - 1 - filt)))
    wv = value_projection.reshape(ring, local, local)
    wo = out_projection.reshape(local, width)
    anywhere = pl.BlockSpec(memory_space=pl.ANY)
    vmem = pltpu.VMEM
    dma = pltpu.SemaphoreType.DMA
    result = pl.pallas_call(
        lambda *refs: kernel(ring, chain, rows, local, groups, min(1, stages - 1), *refs),
        name="two_layers",
        out_shape=jax.ShapeDtypeStruct((rows, local), BF16),
        in_specs=[anywhere] * 7,
        out_specs=pl.BlockSpec(memory_space=pltpu.VMEM),
        scratch_shapes=[
            vmem((2, ring, rows, local), BF16),
            vmem((2, ring, local, local), BF16),
            vmem((2, 1, width), F32),
            vmem((2, *taps.shape), F32),
            vmem((2, 3, 3, local), F32),
            vmem((2, 1, local), F32),
            vmem((2, local, width), BF16),
            vmem((groups * rows, 2 * rows), BF16),
            vmem((groups * rows, local), F32),
            vmem((rows, local), F32),
            vmem((rows, 128), F32),
            vmem((2 * rows + TAIL, local), F32),
            vmem((2 * rows + TAIL, local), F32),
            vmem((2, 2, rows, local), BF16),
            vmem((2, 2, rows, local), BF16),
            vmem((2, 2, TAIL, local), BF16),
            vmem((2, rows, local), F32),
            vmem((2, 2, stages, rows, local), BF16),
            vmem((2, 2, stages, rows, local), BF16),
            vmem((2, 2, stages, rows, local), BF16),
            vmem((2, 2, stages, rows, local), BF16),
            dma,
            dma((6, 2)),
            dma((6,)),
            dma((2, 2, stages, CHUNKS)),
            dma((2, 2, stages, CHUNKS)),
            dma((2, 2, stages)),
            dma((2, 2, stages)),
            dma((2, 2)),
            dma((2, 2)),
            dma((2, 2, stages, CHUNKS)),
            dma((2, 2, stages, CHUNKS)),
            dma((2, 2, stages)),
            dma((2, 2, stages)),
        ],
        compiler_params=pltpu.CompilerParams(
            collective_id=0, has_side_effects=True, vmem_limit_bytes=60 * 1024 * 1024
        ),
    )(activations, wv, norm_gain, taps, short_taps[0], skip_gain, wo)
    return result[None]


def solution(mesh):
    in_specs = (
        P(None, "ctx", "tp"),
        P("section", None),
        P("section", None, "tp"),
        P("section", None, None, "tp"),
        P("section", "tp", None),
        P("section", "tp"),
        P("section", "tp", None),
    )
    out_specs = P("section", "ctx", "tp")
    return jax.shard_map(body, mesh=mesh, in_specs=in_specs, out_specs=out_specs, check_vma=False)
```

```python
import jax
import jax.numpy as jnp
from jax import lax
from jax.experimental import pallas as pl
from jax.experimental.pallas import tpu as pltpu
from jax.sharding import PartitionSpec as P

EPS = 1e-06
CHUNKS = 4
TAIL = 16
MESH = pl.DeviceIdType.MESH
F32 = jnp.float32
BF16 = jnp.bfloat16


def kernel(
    ring, chain, rows, local, groups, lag,
    act, wv_in, gain_in, taps_in, short_in, skip_in, wo_in, out,
    whole, wv, gain, taps, shorts, skips, wo,
    matrix, conv, acc, ssq, qx, vx, qv, halo, tail, scale_out, scale_got, term,
    far_out, far_got, near_out, near_got,
    act_sem, hold_sem, swap_sem,
    agf_s, agf_r, agn_s, agn_r, halo_s, halo_r, rsf_s, rsf_r, rsn_s, rsn_r,
):
    s = lax.axis_index("section")
    c = lax.axis_index("ctx")
    z = lax.axis_index("tp")
    half = ring // 2
    stages = half // 2
    width = ring * local
    group_width = local // groups
    part = rows // CHUNKS
    sign = (1, -1)

    def at_z(d, hops):
        return lax.rem(z + ring + sign[d] * hops, ring)

    ahead = lax.rem(c + 1, chain)
    ahead2 = lax.rem(c + 2, chain)
    behind = lax.rem(c + chain - 1, chain)
    behind2 = lax.rem(c + chain - 2, chain)

    barrier = pltpu.get_barrier_semaphore()
    for there in (
        {"section": 1 - s}, {"tp": at_z(0, 1)}, {"tp": at_z(1, 1)}, {"tp": at_z(0, 2)}, {"tp": at_z(1, 2)},
        {"ctx": ahead}, {"ctx": ahead2}, {"ctx": behind}, {"ctx": behind2},
    ):
        pl.semaphore_signal(barrier, inc=1, device_id=there, device_id_type=MESH)

    own = pltpu.make_async_copy(act.at[s], whole.at[0, z], act_sem)
    own.start()
    weights = (
        (wv_in, wv), (gain_in, gain), (taps_in, taps), (short_in, shorts), (skip_in, skips), (wo_in, wo),
    )
    for index, (source, held) in enumerate(weights):
        pltpu.make_async_copy(source, held.at[s], hold_sem.at[index, s]).start()
    pl.semaphore_wait(barrier, 9)

    def swap(index):
        source, held = weights[index]
        return pltpu.make_async_remote_copy(
            source, held.at[s], swap_sem.at[index], hold_sem.at[index, s],
            device_id={"section": 1 - s}, device_id_type=MESH,
        )

    def ready(layer, *indices):
        for index in indices:
            source, held = weights[index]
            pltpu.make_async_copy(source, held.at[layer], hold_sem.at[index, layer]).wait()

    def piece(q):
        return pl.ds(q * part, part)

    def far_in_gather(d, j):
        return 0 <= j < (stages if d == 0 else stages - 1)

    def far_in_scatter(d, i):
        return (0 if d == 0 else 1) <= i < stages

    def gather_far(layer, d, j, q, received=False):
        block = whole.at[layer, at_z(d, -2 * j - (2 if received else 0)), piece(q)]
        return pltpu.make_async_remote_copy(
            block, block, agf_s.at[layer, d, j, q], agf_r.at[layer, d, j, q],
            device_id={"tp": at_z(d, 2)}, device_id_type=MESH,
        )

    def gather_near(layer, d, j, received=False):
        block = whole.at[layer, at_z(d, -2 * j - (1 if received else 0))]
        return pltpu.make_async_remote_copy(
            block, block, agn_s.at[layer, d, j], agn_r.at[layer, d, j],
            device_id={"tp": at_z(d, 1)}, device_id_type=MESH,
        )

    def scatter_far(layer, d, i, q):
        return pltpu.make_async_remote_copy(
            far_out.at[layer, d, i, piece(q)], far_got.at[layer, d, i, piece(q)],
            rsf_s.at[layer, d, i, q], rsf_r.at[layer, d, i, q],
            device_id={"tp": at_z(d, 2)}, device_id_type=MESH,
        )

    def scatter_near(layer, d, i):
        return pltpu.make_async_remote_copy(
            near_out.at[layer, d, i], near_got.at[layer, d, i],
            rsn_s.at[layer, d, i], rsn_r.at[layer, d, i],
            device_id={"tp": at_z(d, 1)}, device_id_type=MESH,
        )

    def to_next(source, target, layer, index):
        return pltpu.make_async_remote_copy(
            source, target, halo_s.at[layer, index], halo_r.at[layer, index],
            device_id={"ctx": ahead}, device_id_type=MESH,
        )

    def block_copy(layer):
        return to_next(whole.at[layer, z], halo.at[layer, 0], layer, 0)

    def halo_copy(layer):
        return to_next(qv.at[layer, 1], halo.at[layer, 1], layer, 2)

    def scale_copy(layer):
        return to_next(scale_out.at[layer], scale_got.at[layer], layer, 3)

    def tail_copy(layer):
        return pltpu.make_async_remote_copy(
            qv.at[layer, :, pl.ds(rows - TAIL, TAIL)], tail.at[layer],
            halo_s.at[layer, 1], halo_r.at[layer, 1],
            device_id={"ctx": ahead2}, device_id_type=MESH,
        )

    own.wait()
    for layer in range(2):
        for q in range(CHUNKS):
            for d in range(2):
                if far_in_gather(d, 0):
                    gather_far(layer, d, 0, q).start()
        for d in range(2):
            gather_near(layer, d, 0).start()
        block_copy(layer).start()
        if layer == 0:
            for index in range(6):
                swap(index).start()
        acc[...] = jnp.zeros_like(acc)
        ssq[...] = jnp.zeros_like(ssq)

        def gain_of(o, layer=layer):
            return gain[layer, :, pl.ds(pl.multiple_of(o * local, local), local)]

        def project(o, layer=layer):
            x = whole[layer, o].astype(F32)
            squared = x * x
            lanes = squared[:, :128]
            for at in range(128, local, 128):
                lanes = lanes + squared[:, at : at + 128]
            ssq[...] += lanes
            normed = (x * gain_of(o)).astype(BF16)
            acc[...] += jnp.dot(normed, wv[layer, o], preferred_element_type=F32)

        def build(g, layer=layer):
            base = jnp.broadcast_to(taps[layer, g : g + 1, :], (rows, 2 * rows))
            turned = pltpu.roll(base, 0, 1, stride=1, stride_axis=0)
            matrix[g * rows : (g + 1) * rows, :] = turned.astype(BF16)

        pending = [(z, None)]
        built = 0
        waited = False
        for j in range(stages):
            for q in range(CHUNKS):
                for d in range(2):
                    if far_in_gather(d, j):
                        gather_far(layer, d, j, q, received=True).wait_recv()
                        if far_in_gather(d, j + 1):
                            gather_far(layer, d, j + 1, q).start()
            for d in range(2):
                if far_in_gather(d, j):
                    if j + 1 < stages:
                        gather_near(layer, d, j + 1).start()
                    pending.append((at_z(d, -2 * j - 2), None))
                pending.append((at_z(d, -2 * j - 1), gather_near(layer, d, j, received=True)))
            if layer == 0 and j < lag:
                continue
            if not waited:
                ready(layer, 0, 1, 2)
                waited = True
            count = 8 if j + 1 < stages else len(pending)
            for o, copy in pending[:count]:
                if copy is not None:
                    copy.wait_recv()
                project(o)
            pending = pending[count:]
            goal = groups * (j + 1) // stages
            for g in range(built, goal):
                build(g)
            built = goal

        def short(i, which, layer=layer):
            return shorts[layer, i, which : which + 1, :]

        def featured(which, x, start, count):
            return (
                short(0, which) * x[start : start + count, :]
                + short(1, which) * x[start - 1 : start - 1 + count, :]
                + short(2, which) * x[start - 2 : start - 2 + count, :]
            )

        scale = lax.rsqrt(jnp.sum(ssq[...], axis=1, keepdims=True) / width + EPS)
        values = (acc[...] * scale).astype(BF16)
        qv[layer, 1] = values
        halo_copy(layer).start()
        eye = lax.broadcasted_iota(jnp.int32, (rows, rows), 0) == lax.broadcasted_iota(
            jnp.int32, (rows, rows), 1
        )
        scale_row = jnp.sum(jnp.where(eye, scale, 0.0), axis=0, keepdims=True)
        scale_out[layer] = jnp.broadcast_to(scale_row, (8, rows))
        scale_copy(layer).start()

        def query_of(block, by):
            normed = (block.astype(F32) * gain_of(z)).astype(BF16)
            return (normed.astype(F32) * by).astype(BF16)

        query = query_of(whole[layer, z], scale)
        qv[layer, 0] = query
        tail_copy(layer).start()
        qx[TAIL + rows :, :] = query.astype(F32)
        vx[TAIL + rows :, :] = values.astype(F32)
        ready(layer, 3, 4)
        block_copy(layer).wait_recv()
        scale_copy(layer).wait_recv()
        scale_behind = jnp.sum(jnp.where(eye, scale_got[layer, :1, :], 0.0), axis=1, keepdims=True)
        query_behind = query_of(halo[layer, 0], scale_behind)
        halo_copy(layer).wait_recv()
        tail_copy(layer).wait_recv()
        for index, x, block in ((0, qx, query_behind), (1, vx, halo[layer, 1])):
            x[TAIL : TAIL + rows, :] = jnp.where(c > 0, block.astype(F32), 0.0)
            x[:TAIL, :] = jnp.where(c > 1, tail[layer, index].astype(F32), 0.0)
        product = (
            featured(1, qx, TAIL, 2 * rows) * featured(2, vx, TAIL, 2 * rows)
        ).astype(BF16)
        conv[...] = jnp.dot(matrix[...], product, preferred_element_type=F32)
        group_of = lax.broadcasted_iota(jnp.int32, (rows, local), 1) // group_width
        filtered = conv[:rows, :]
        for g in range(1, groups):
            filtered = jnp.where(group_of == g, conv[g * rows : (g + 1) * rows, :], filtered)
        mixed = filtered + skips[layer] * product[rows:, :].astype(F32)
        gated = (featured(0, qx, TAIL + rows, rows) * mixed).astype(BF16)
        ready(layer, 5)

        def terms(dest, layer=layer, gated=gated):
            columns = pl.ds(pl.multiple_of(dest * local, local), local)
            return jnp.dot(gated, wo[layer, :, columns], preferred_element_type=F32)

        def send_near(i, layer=layer):
            for d in range(2):
                near_out[layer, d, i] = terms(at_z(d, half - 2 * i - 1)).astype(BF16)
                scatter_near(layer, d, i).start()

        far_out[layer, 0, 0] = terms(at_z(0, half)).astype(BF16)
        for q in range(CHUNKS):
            scatter_far(layer, 0, 0, q).start()
        send_near(0)
        for i in range(1, stages):
            for d in range(2):
                term[d] = terms(at_z(d, half - 2 * i))
            send_near(i)
            for d in (1, 0):
                scatter_near(layer, d, i - 1).wait_recv()
            for q in range(CHUNKS):
                for d in (1, 0):
                    total = term[d, piece(q)] + near_got[layer, d, i - 1, piece(q)].astype(F32)
                    if far_in_scatter(d, i - 1):
                        scatter_far(layer, d, i - 1, q).wait_recv()
                        total = total + far_got[layer, d, i - 1, piece(q)].astype(F32)
                    far_out[layer, d, i, piece(q)] = total.astype(BF16)
                    scatter_far(layer, d, i, q).start()
        term[0] = whole[layer, z].astype(F32)
        term[1] = terms(z)
        for d in range(2):
            scatter_near(layer, d, stages - 1).wait_recv()
        for q in range(CHUNKS):
            summed = term[1, piece(q)]
            for d in range(2):
                summed = summed + near_got[layer, d, stages - 1, piece(q)].astype(F32)
                if far_in_scatter(d, stages - 1):
                    scatter_far(layer, d, stages - 1, q).wait_recv()
                    summed = summed + far_got[layer, d, stages - 1, piece(q)].astype(F32)
            result = (term[0, piece(q)] + summed).astype(BF16)
            if layer == 0:
                whole[1, z, piece(q)] = result
            else:
                out[piece(q), :] = result

    for index in range(6):
        swap(index).wait_send()
    for layer in range(2):
        block_copy(layer).wait_send()
        halo_copy(layer).wait_send()
        scale_copy(layer).wait_send()
        tail_copy(layer).wait_send()
        for d in range(2):
            for j in range(stages):
                gather_near(layer, d, j).wait_send()
                scatter_near(layer, d, j).wait_send()
                for q in range(CHUNKS):
                    if far_in_gather(d, j):
                        gather_far(layer, d, j, q).wait_send()
                    if far_in_scatter(d, j):
                        scatter_far(layer, d, j, q).wait_send()


def body(
    activations, norm_gain, value_projection, short_taps, long_taps, skip_gain, out_projection
):
    ring = lax.axis_size("tp")
    chain = lax.axis_size("ctx")
    rows, local = activations.shape[1:]
    width = value_projection.shape[1]
    groups, filt = long_taps.shape[1:]
    stages = ring // 4
    turned = jnp.flip(long_taps[0].astype(F32), axis=1)
    taps = jnp.pad(turned, ((0, 0), (1, local - 1 - filt)))
    wv = value_projection.reshape(ring, local, local)
    wo = out_projection.reshape(local, width)
    anywhere = pl.BlockSpec(memory_space=pl.ANY)
    vmem = pltpu.VMEM
    dma = pltpu.SemaphoreType.DMA
    result = pl.pallas_call(
        lambda *refs: kernel(ring, chain, rows, local, groups, min(1, stages - 1), *refs),
        name="two_layers",
        out_shape=jax.ShapeDtypeStruct((rows, local), BF16),
        in_specs=[anywhere] * 7,
        out_specs=pl.BlockSpec(memory_space=pltpu.VMEM),
        scratch_shapes=[
            vmem((2, ring, rows, local), BF16),
            vmem((2, ring, local, local), BF16),
            vmem((2, 1, width), F32),
            vmem((2, *taps.shape), F32),
            vmem((2, 3, 3, local), F32),
            vmem((2, 1, local), F32),
            vmem((2, local, width), BF16),
            vmem((groups * rows, 2 * rows), BF16),
            vmem((groups * rows, local), F32),
            vmem((rows, local), F32),
            vmem((rows, 128), F32),
            vmem((2 * rows + TAIL, local), F32),
            vmem((2 * rows + TAIL, local), F32),
            vmem((2, 2, rows, local), BF16),
            vmem((2, 2, rows, local), BF16),
            vmem((2, 2, TAIL, local), BF16),
            vmem((2, 8, rows), F32),
            vmem((2, 8, rows), F32),
            vmem((2, rows, local), F32),
            vmem((2, 2, stages, rows, local), BF16),
            vmem((2, 2, stages, rows, local), BF16),
            vmem((2, 2, stages, rows, local), BF16),
            vmem((2, 2, stages, rows, local), BF16),
            dma,
            dma((6, 2)),
            dma((6,)),
            dma((2, 2, stages, CHUNKS)),
            dma((2, 2, stages, CHUNKS)),
            dma((2, 2, stages)),
            dma((2, 2, stages)),
            dma((2, 4)),
            dma((2, 4)),
            dma((2, 2, stages, CHUNKS)),
            dma((2, 2, stages, CHUNKS)),
            dma((2, 2, stages)),
            dma((2, 2, stages)),
        ],
        compiler_params=pltpu.CompilerParams(
            collective_id=0, has_side_effects=True, vmem_limit_bytes=60 * 1024 * 1024
        ),
    )(activations, wv, norm_gain, taps, short_taps[0], skip_gain, wo)
    return result[None]


def solution(mesh):
    in_specs = (
        P(None, "ctx", "tp"),
        P("section", None),
        P("section", None, "tp"),
        P("section", None, None, "tp"),
        P("section", "tp", None),
        P("section", "tp"),
        P("section", "tp", None),
    )
    out_specs = P("section", "ctx", "tp")
    return jax.shard_map(body, mesh=mesh, in_specs=in_specs, out_specs=out_specs, check_vma=False)
```
